32 devices in a mesh: grp: 4 (over y, core), span: 8 (over z, x).
Axes of the slice: x: 2, y: 2, z: 4, core: 2. Of those that a mesh axis runs over, the one named last changes fastest.
Arguments:
- record: float32 [131072, 128], P(('grp', 'span')), may hold values from -96 to 96, as said below
Outputs:
- triangle: float32 [512, 512], replicated
- operator: float32 [512, 512], replicated
The draws below stay inside these ranges and needn't reach their ends.
Inputs may be any that keep to these rules, and one draw needn't show every extreme that they name: `record`: Real-valued probe samples.
All inputs are finite; a program needn't handle non-finite values.
Results may differ from the reference program's by a relative error of at most 0.0003.
Values sent between devices are 32-bit elements; how exact they have to be, the bound alone decides.
A program may use at most 64 MiB of HBM per device.

```python
import jax
import jax.numpy as jnp
from jax import lax

COMPS = 128
LAGS = 4
DELAY = 1024
ROWS_DEV = 4096
COLS = 512
SAMPLES = 131072
HROWS = 127999


def draw_record(key, part):
    keys = jax.random.split(jax.random.fold_in(key, 17), 5)
    colscale = jnp.exp(jax.random.uniform(keys[0], (1, COMPS), jnp.float32) * 2.302585)
    freq = jax.random.randint(keys[1], (1, COMPS), 1, 32768)
    phase = jax.random.randint(keys[2], (1, COMPS), 0, 65536)
    times = jnp.arange(SAMPLES, dtype=jnp.int32)[:, None]
    turns = (freq * (times % 65536) + phase) % 65536
    wave = 0.8 * jnp.sin(turns.astype(jnp.float32) * (6.2831853 / 65536.0))
    envelope = 0.6 + 1.2 * times.astype(jnp.float32) / SAMPLES
    noise = jax.random.truncated_normal(keys[4], -4.0, 4.0, (SAMPLES, COMPS), jnp.float32)
    return (colscale * envelope * (noise + wave)).astype(jnp.float32)


def setup_inputs(seed: int = 0) -> dict:
    streams_of = jax.random.split(jax.random.key(seed), 2)
    return {
        "record": draw_record(jax.random.fold_in(streams_of[1], 71), 0),
    }


def block_terms(padded, start, count):
    lead = (LAGS - 1) * DELAY + 1
    ext = lax.dynamic_slice_in_dim(padded, start, count + lead, 0)
    hank = jnp.concatenate([ext[k * DELAY:k * DELAY + count + 1] for k in range(LAGS)], 1)
    times = start + jnp.arange(count, dtype=jnp.int32)
    weight = jnp.where(times < HROWS, 1.0, 0.0) - 0.5 * jnp.where(times == 0, 1.0, 0.0) - 0.5 * jnp.where(times == HROWS, 1.0, 0.0)
    weight = weight.astype(jnp.float32)
    inside = jnp.where(times < HROWS, 1.0, 0.0).astype(jnp.float32)
    head = hank[:count]
    gram = lax.dot_general((head * weight[:, None]).astype(jnp.float32), head.astype(jnp.float32), (((0,), (0,)), ((), ())), precision=lax.Precision.HIGHEST, preferred_element_type=jnp.float32)
    cross = lax.dot_general((head * inside[:, None]).astype(jnp.float32), hank[1:count + 1].astype(jnp.float32), (((0,), (0,)), ((), ())), precision=lax.Precision.HIGHEST, preferred_element_type=jnp.float32)
    return (gram, cross)

def reference(record):
    lead = (LAGS - 1) * DELAY + 1
    padded = jnp.concatenate([record, jnp.zeros((lead, COMPS), jnp.float32)], 0)
    blocks = SAMPLES // ROWS_DEV

    def step(carry, index):
        gram, cross = block_terms(padded, (index * ROWS_DEV).astype(jnp.int32), ROWS_DEV)
        return ((carry[0] + gram, carry[1] + cross), None)
    zeros = jnp.zeros((COLS, COLS), jnp.float32)
    (gram, cross), unused = lax.scan(step, (zeros, zeros), jnp.arange(blocks, dtype=jnp.int32))
    lower = jnp.linalg.cholesky(gram / HROWS)
    middle = jax.scipy.linalg.solve_triangular(lower, cross / HROWS, lower=True)
    operator = jax.scipy.linalg.solve_triangular(lower, middle.T, lower=True).T
    return (lower.T, operator)
```

```python
import functools

import jax
import jax.numpy as jnp
from jax import lax
from jax.experimental import pallas as pl
from jax.experimental.pallas import tpu as pltpu
from jax.sharding import PartitionSpec as P

LAGS = 4
DELAY = 1024
AXES = ("grp", "span")
HIGH = lax.Precision.HIGHEST


def contract(left, right, dims, precision=None):
    return lax.dot_general(
        left, right, (dims, ((), ())), precision=precision,
        preferred_element_type=jnp.float32,
    )


def factor(block):
    n = block.shape[0]
    groups = n // 8
    lane = lax.broadcasted_iota(jnp.int32, (8, n), 1)
    sub = lax.broadcasted_iota(jnp.int32, (8, n), 0)
    a = [block[8 * g:8 * g + 8, :] for g in range(groups)]
    b = [jnp.where(lane == sub + 8 * g, 1.0, 0.0) for g in range(groups)]
    for k in range(n):
        g, r = divmod(k, 8)
        inverse = 1.0 / a[g][r:r + 1, k:k + 1]
        row = a[g][r:r + 1, :] * inverse
        brow = b[g][r:r + 1, :] * inverse
        for h in range(g, groups):
            if h == g and r == 7:
                continue
            column = jnp.broadcast_to(a[h][:, k:k + 1], (8, n))
            if h == g:
                column = jnp.where(sub > r, column, 0.0)
            a[h] = a[h] - column * row
            b[h] = b[h] - column * brow
    for g in range(groups):
        here = lane == sub + 8 * g
        pivot = jnp.sum(jnp.where(here, a[g], 0.0), axis=1, keepdims=True)
        scale = 1.0 / jnp.sqrt(pivot)
        a[g] = jnp.where(lane >= sub + 8 * g, a[g] * scale, 0.0)
        b[g] = b[g] * scale
    return jnp.concatenate(a, 0), jnp.concatenate(b, 0)


def solve_kernel(comps, scale, gram_ref, cross_ref, tri_ref, op_ref, work, inverses):
    size = LAGS * comps
    for i in range(LAGS):
        rows = pl.ds(i * comps, comps)
        work[i, :, pl.ds(0, size)] = gram_ref[rows, :] * scale
        work[i, :, pl.ds(size, size)] = cross_ref[rows, :] * scale
        if i:
            tri_ref[rows, pl.ds(0, i * comps)] = jnp.zeros((comps, i * comps), jnp.float32)

    def step(i, carry):
        at = pl.multiple_of(i * comps, comps)
        upper, inverse = factor(work[i, :, pl.ds(at, comps)])
        inverses[i] = inverse
        work[i] = contract(inverse, work[i], ((1,), (0,)), HIGH)
        work[i, :, pl.ds(at, comps)] = upper

        def update(j, carry):
            to = pl.multiple_of(j * comps, comps)
            work[j] = work[j] - contract(work[i, :, pl.ds(to, comps)], work[i], ((0,), (0,)), HIGH)
            return carry
        lax.fori_loop(i + 1, LAGS, update, 0)
        return carry
    lax.fori_loop(0, LAGS, step, 0)

    for i in range(LAGS):
        for j in range(i, LAGS):
            tri_ref[pl.ds(i * comps, comps), pl.ds(j * comps, comps)] = work[i, :, pl.ds(j * comps, comps)]
    for b in range(LAGS):
        rest = jnp.concatenate(
            [work[i, :, pl.ds((LAGS + b) * comps, comps)] for i in range(LAGS)], 0)
        if b:
            rest = rest - contract(
                op_ref[:, pl.ds(0, b * comps)],
                tri_ref[pl.ds(0, b * comps), pl.ds(b * comps, comps)], ((1,), (0,)), HIGH)
        op_ref[:, pl.ds(b * comps, comps)] = contract(rest, inverses[b], ((1,), (1,)), HIGH)


def shifted(value, axis, steps):
    count = lax.axis_size(axis)
    leading, last = (max(0, -steps), min(count, count - steps))
    return lax.ppermute(value, axis, [(source, source + steps) for source in range(leading, last)])


def inner_rows(left, right):
    return lax.dot_general(
        left,
        right,
        (((0,), (0,)), ((), ())),
        precision=lax.Precision.HIGHEST,
        preferred_element_type=jnp.float32,
    )


def on_device(record):
    count = record.shape[0]
    lead = (LAGS - 1) * DELAY + 1
    following = shifted(record[:lead], ("grp", "span"), -1)
    ext = jnp.concatenate([record, following], 0)
    hank = jnp.concatenate([ext[k * DELAY : k * DELAY + count + 1] for k in range(LAGS)], 1)
    devices = lax.axis_size(("grp", "span"))
    last_row = count * devices - lead
    times = lax.axis_index(("grp", "span")) * count + jnp.arange(count, dtype=jnp.int32)
    weight = (
        jnp.where(times < last_row, 1.0, 0.0)
        - 0.5 * jnp.where(times == 0, 1.0, 0.0)
        - 0.5 * jnp.where(times == last_row, 1.0, 0.0)
    )
    weight = weight.astype(jnp.float32)
    inside = jnp.where(times < last_row, 1.0, 0.0).astype(jnp.float32)
    head = hank[:count]
    weighted = head * weight[:, None]
    cross = inner_rows(head * inside[:, None], hank[1 : count + 1])
    scale = 1.0 / last_row
    gram = inner_rows(weighted, head)
    gram, cross = lax.psum((gram, cross), ("grp", "span"))
    comps = record.shape[1]
    size = LAGS * comps
    vmem = pl.BlockSpec(memory_space=pltpu.VMEM)
    return pl.pallas_call(
        functools.partial(solve_kernel, comps, scale),
        out_shape=(jax.ShapeDtypeStruct((size, size), jnp.float32),) * 2,
        in_specs=[vmem] * 2, out_specs=(vmem, vmem),
        scratch_shapes=[
            pltpu.VMEM((LAGS, comps, 2 * size), jnp.float32),
            pltpu.VMEM((LAGS, comps, comps), jnp.float32),
        ],
        compiler_params=pltpu.CompilerParams(vmem_limit_bytes=48 << 20),
    )(gram, cross)


def solution(mesh):
    placed = (P(AXES, None),)
    return jax.shard_map(
        on_device, mesh=mesh, in_specs=placed, out_specs=(P(), P()), check_vma=False
    )
```
